32 devices in a mesh: groups: 1, pts: 32 (over z, y, x, core).
Axes of the slice: x: 2, y: 2, z: 4, core: 2. Of those that a mesh axis runs over, the one named last changes fastest.
Arguments:
- residual_cols: bfloat16 [16384, 256], P(('groups', 'pts')), may hold values from -6 to 6
- leaf_inverse: bfloat16 [16384, 128], P(('groups', 'pts'))
- basis_left: float32 [7, 16384, 128], P(None, ('groups', 'pts')), may hold values from -0.15625 to 0.15625
- basis_right: float32 [7, 16384, 128], P(None, ('groups', 'pts'))
- point_pos: float32 [16384], replicated, may hold values from 0 to 16, as said below
- map_pos: float32 [2048], P('pts'), may hold values from 0 to 16, as said below
- prior_map: bfloat16 [2048, 256], P(('groups', 'pts')), may hold values from -6 to 6
- block_first: int32 [32, 32], replicated, may hold values from 0 to 2, as said below
- block_count: int32 [32, 32], replicated, may hold values from 0 to 2, as said below
Outputs:
- solved_cols: float32 [16384, 256], P(('groups', 'pts'))
- sample_map: float32 [2048, 256], P(('groups', 'pts'))
The draws below stay inside these ranges and needn't reach their ends.
Inputs may be any that keep to these rules, and one draw needn't show every extreme that they name: `block_count`: at most 2; the listed blocks of tile d from source s include every block of s that has a point within distance 1 of some map point of tile d; in every draw some tile owner receives 2 blocks from every source; the totals per owner differ strongly between owners. `block_first`: listed blocks stay inside the source's 4 blocks. `point_pos`: points of one leaf block lie in increasing order within an interval of length 1. `map_pos`: the map points of one tile lie within an interval of length at most 6.
All inputs are finite; a program needn't handle non-finite values.
Results may differ from the reference program's by a relative error of at most 0.003.
Values may be sent and summed in bfloat16 or wider, within the bound.
A program may use at most 128 MiB of HBM per device.

```python
import jax
import jax.numpy as jnp
from jax import lax

MAP_DEV = 64
SAMPLES = 256
RANK = 128
LEAF = 128
LEVELS = 7
CAP = 2
BLK_DEV = 4
POINTS = 16384
MAPS = 2048
N_PTS = 32


def draw_leaf_inverse(key, part):
    first_key, second_key = jax.random.split(key)
    row_place = jnp.arange(POINTS)[:, None] % LEAF
    column_place = jnp.arange(LEAF)[None, :]
    diagonal = jnp.exp(jax.random.uniform(first_key, (POINTS, LEAF), minval=jnp.log(0.5), maxval=jnp.log(2.0)))
    off_diagonal = jax.random.normal(second_key, (POINTS, LEAF)) * (0.5 / LEAF ** 0.5)
    return jnp.where(row_place == column_place, diagonal, off_diagonal).astype(jnp.float32).astype(jnp.bfloat16)


def draw_basis_right(key, part):
    level_ids = jnp.arange(LEVELS)[:, None, None].astype(jnp.float32)
    half_sizes = POINTS / 2.0 / 2.0 ** level_ids
    base = jax.random.normal(key, (LEVELS, POINTS, RANK))
    return (base / jnp.sqrt(half_sizes)).astype(jnp.float32)


def chord_layout(key):
    offset_key = jax.random.fold_in(key, 21)
    level_key = jax.random.fold_in(key, 22)
    forced_key = jax.random.fold_in(key, 23)
    start_key = jax.random.fold_in(key, 24)
    cell_total = 4 * BLK_DEV
    offsets = jax.random.randint(offset_key, (N_PTS,), 0, 4).astype(jnp.int32)
    level_draw = jax.random.randint(level_key, (N_PTS,), 0, 8)
    widths = jnp.where(level_draw < 5, 1, jnp.where(level_draw < 7, 3, 6)).astype(jnp.int32)
    forced = jax.random.randint(forced_key, (), 0, N_PTS)
    widths = jnp.where(jnp.arange(N_PTS) == forced, 6, widths).astype(jnp.int32)
    starts = jax.random.randint(start_key, (N_PTS,), 1, cell_total - 6).astype(jnp.int32)
    return (offsets, widths, starts)


def table_pair(key):
    offsets, widths, starts = chord_layout(key)
    lower = (starts - 1)[:, None] - offsets[None, :]
    upper = (starts + widths)[:, None] - offsets[None, :]
    first_live = jnp.maximum((lower + 3) // 4, 0)
    last_live = jnp.minimum(upper // 4, BLK_DEV - 1)
    live_total = jnp.maximum(last_live - first_live + 1, 0)
    first = jnp.minimum(first_live, BLK_DEV - CAP)
    count = jnp.where(live_total > 0, last_live - first + 1, 0)
    return (first.astype(jnp.int32), count.astype(jnp.int32))


def draw_block_first(key, part):
    return table_pair(key)[0]


def draw_block_count(key, part):
    return table_pair(key)[1]


def draw_point_pos(key, part):
    offsets, widths, starts = chord_layout(key)
    gap_key = jax.random.fold_in(key, 31)
    gaps = jax.random.uniform(gap_key, (N_PTS, BLK_DEV, LEAF), minval=0.2, maxval=1.0)
    running = jnp.cumsum(gaps, axis=2)
    inside = 0.999 * (running - gaps[:, :, :1]) / running[:, :, -1:]
    cells = (offsets[:, None] + 4 * jnp.arange(BLK_DEV)[None, :]).astype(jnp.float32)
    return (cells[:, :, None] + inside).reshape(POINTS).astype(jnp.float32)


def draw_map_pos(key, part):
    offsets, widths, starts = chord_layout(key)
    spot_key = jax.random.fold_in(key, 32)
    spots = jax.random.uniform(spot_key, (N_PTS, MAP_DEV), minval=0.0, maxval=0.999)
    placed = starts.astype(jnp.float32)[:, None] + widths.astype(jnp.float32)[:, None] * spots
    return placed.reshape(MAPS).astype(jnp.float32)


def level_of(own_key, shape, shards, low, largest):
    level, own = 1.0, jax.random.fold_in(own_key, 6)
    for position, parts in shards:
        steps = jnp.exp(jax.random.uniform(jax.random.fold_in(own, position), (parts,), jnp.float32, low / len(shards), largest / len(shards)))
        level = level * jnp.repeat(steps, shape[position] // parts).reshape([-1 if axis == position else 1 for axis in range(len(shape))])
    return level


def noise(rng, shape, spread, reach, pieces=(), kind=jnp.bfloat16):
    entries = jax.random.normal(rng, shape, jnp.float32) * spread
    if len(pieces) > 0:
        entries = level_of(rng, shape, pieces, -0.22, 0.18) * entries
    return jnp.clip(entries, min=-reach, max=reach).astype(kind)


def setup_inputs(seed: int = 0, part: int = 0) -> dict:
    key_of = jax.random.split(jax.random.key(seed), 10)
    part_splits = jax.random.split(jax.random.fold_in(key_of[9], part), 10)
    return {
        "residual_cols": noise(part_splits[0], (POINTS, SAMPLES), 1.0, 6.0, ((0, 32),)),
        "leaf_inverse": draw_leaf_inverse(jax.random.fold_in(jax.random.fold_in(key_of[9], part), 71), part),
        "basis_left": noise(part_splits[2], (LEVELS, POINTS, RANK), (10 * RANK) ** -0.5, 0.15625, ((1, 32),), jnp.float32),
        "basis_right": draw_basis_right(jax.random.fold_in(jax.random.fold_in(key_of[9], part), 71), part),
        "point_pos": draw_point_pos(jax.random.fold_in(key_of[9], 71), part),
        "map_pos": draw_map_pos(jax.random.fold_in(key_of[9], 71), part),
        "prior_map": noise(part_splits[6], (MAPS, SAMPLES), 1.0, 6.0, ((0, 32),)),
        "block_first": draw_block_first(jax.random.fold_in(key_of[9], 71), part),
        "block_count": draw_block_count(jax.random.fold_in(key_of[9], 71), part),
    }


amplitude = 0.2
highest = lax.Precision.HIGHEST


def wendland(distance):
    scaled = jnp.minimum(jnp.abs(distance) * (2.0 * LEAF), 1.0)
    return (1.0 - scaled) ** 4 * (1.0 + 4.0 * scaled)


def reference(residual_cols, leaf_inverse, basis_left, basis_right, point_pos, map_pos, prior_map, block_first, block_count):
    block_total = POINTS // LEAF
    inverses = leaf_inverse.reshape(block_total, LEAF, LEAF).astype(jnp.float32)
    right_side = residual_cols.reshape(block_total, LEAF, SAMPLES).astype(jnp.float32)
    solved = jnp.einsum("bij,bjs->bis", inverses, right_side, precision=highest).reshape(POINTS, SAMPLES)
    for level_index in reversed(range(LEVELS)):
        half_size = POINTS // 2 ** (level_index + 1)
        node_count = POINTS // (2 * half_size)
        coeff_view = solved.reshape(node_count, 2, half_size, SAMPLES)
        right_view = basis_right[level_index].reshape(node_count, 2, half_size, RANK)
        left_view = basis_left[level_index].reshape(node_count, 2, half_size, RANK)
        projected = jnp.einsum("nhpr,nhps->nhrs", right_view, coeff_view, precision=highest)
        sibling = projected[:, ::-1]
        update = jnp.einsum("nhpr,nhrs->nhps", left_view, sibling, precision=highest)
        solved = solved + update.reshape(POINTS, SAMPLES)
    coeffs = solved.astype(jnp.bfloat16)
    coeff_blocks = coeffs.reshape(N_PTS, BLK_DEV, LEAF, SAMPLES)
    position_blocks = point_pos.reshape(N_PTS, BLK_DEV, LEAF)
    sources = jnp.arange(N_PTS, dtype=jnp.int32)[:, None]
    slot_range = jnp.arange(CAP, dtype=jnp.int32)[None, :]

    def owner_map(owner):
        slot_index = block_first[owner][:, None] + slot_range
        live = slot_range < block_count[owner][:, None]
        data = coeff_blocks[sources, slot_index]
        positions = position_blocks[sources, slot_index]
        targets = lax.dynamic_slice_in_dim(map_pos, owner * MAP_DEV, MAP_DEV)
        kernel = amplitude * wendland(targets[:, None, None, None] - positions[None])
        weights = jnp.where(live[None, :, :, None], kernel, 0.0).astype(jnp.bfloat16)
        return jnp.dot(weights.reshape(MAP_DEV, -1), data.reshape(-1, SAMPLES), preferred_element_type=jnp.float32)

    terms = lax.map(owner_map, jnp.arange(N_PTS, dtype=jnp.int32))
    sample_map = prior_map.astype(jnp.float32) + terms.reshape(MAPS, SAMPLES)
    return solved, sample_map
```

```python
import functools

import jax
import jax.numpy as jnp
from jax import lax
from jax.experimental import pallas as pl
from jax.experimental.pallas import tpu as pltpu
from jax.sharding import PartitionSpec as P

AMPLITUDE = 0.2
FAR = -1e6
f32 = jnp.float32
bf16 = jnp.bfloat16


def split(value):
    high = value.astype(bf16)
    return high, (value - high.astype(f32)).astype(bf16)


def mm(a, b):
    return jnp.dot(a, b, preferred_element_type=f32)


def mm3(a, b):
    return mm(a[0], b[0]) + mm(a[0], b[1]) + mm(a[1], b[0])


def kernel(
    n,
    leaf,
    res_ref,
    inv_ref,
    bl_ref,
    br_ref,
    pp_ref,
    mp_ref,
    prior_ref,
    first_ref,
    count_ref,
    out_ref,
    map_ref,
    xs,
    rth,
    rtl,
    lh,
    ll,
    gf,
    gs,
    gr,
    tf,
    ts,
    tr,
    cbuf,
    co,
    mpb,
    wts,
    acc,
    ms,
    mr,
    send_sem,
    recv_sem,
):
    rows, samples = res_ref.shape
    rank = bl_ref.shape[2]
    levels = bl_ref.shape[0]
    half = samples // 2
    depth = n.bit_length() - 1
    tile = prior_ref.shape[0]
    me = lax.axis_index("pts")
    bits = [lax.rem(me // 2**k, 2) for k in range(depth)]
    partners = [me + 2**k * (1 - 2 * bits[k]) for k in range(depth)]
    par = bits[0]
    started = []

    def remote(src, dst, k):
        index = len(started)
        copy = pltpu.make_async_remote_copy(
            src_ref=src,
            dst_ref=dst,
            send_sem=send_sem.at[index],
            recv_sem=recv_sem.at[index],
            device_id={"pts": partners[k]},
            device_id_type=pl.DeviceIdType.MESH,
        )
        copy.start()
        started.append(copy)
        return copy

    barrier = pltpu.get_barrier_semaphore()
    for k in range(depth):
        pl.semaphore_signal(
            barrier, inc=1, device_id={"pts": partners[k]}, device_id_type=pl.DeviceIdType.MESH
        )

    pairs = [m * (m + 1) // 2 for m in range(depth)]
    g_off, t_off, m_off = [], [], []
    g_at = t_at = m_at = 0
    for k in range(depth):
        m = depth - 1 - k
        g_off.append(g_at)
        t_off.append(t_at)
        m_off.append(m_at)
        g_at += pairs[m]
        t_at += m + 1
        m_at += n // 2 ** (k + 1) * tile

    mpb[0] = mp_ref[0]
    for l in range(depth):
        high, low = split(br_ref[l].T)
        rth[l * rank : (l + 1) * rank, :] = high
        rtl[l * rank : (l + 1) * rank, :] = low
        high, low = split(bl_ref[l])
        lh[:, l * rank : (l + 1) * rank] = high
        ll[:, l * rank : (l + 1) * rank] = low
    at = 0
    for m in range(depth - 1, 0, -1):
        product = mm(rth[: m * rank, :], lh[:, m * rank : (m + 1) * rank])
        product = product.reshape(m, rank, rank)
        gf[at : at + m] = product
        gs[at : at + m] = product.astype(bf16)
        at += m

    pl.semaphore_wait(barrier, depth)

    def start_g(k):
        size = pairs[depth - 1 - k]
        view = pl.ds(g_off[k], size)
        return remote(gs.at[view], gr.at[view], k)

    def start_mp(k):
        return remote(mpb.at[pl.ds(0, 2**k)], mpb.at[pl.ds(2**k, 2**k)], k)

    mp_copy = start_mp(0)
    g_copy = start_g(0) if depth > 1 else None

    for b in range(rows // leaf):
        part = mm(inv_ref[b * leaf : (b + 1) * leaf, :], res_ref[b * leaf : (b + 1) * leaf, :])
        xs[b * leaf : (b + 1) * leaf, :] = part
    total_rows = rows * n
    for level in range(levels - 1, depth - 1, -1):
        size = total_rows // 2 ** (level + 1)
        count = rows // size
        projected = []
        for a in range(count):
            view = slice(a * size, (a + 1) * size)
            projected.append(split(mm3(split(br_ref[level, view, :].T), split(xs[view, :]))))
        for a in range(count):
            view = slice(a * size, (a + 1) * size)
            xs[view, :] += mm3(split(bl_ref[level, view, :]), projected[a ^ 1])

    mp_copy.wait_recv()
    mp_next = 1
    if mp_next < depth:
        mp_copy = start_mp(mp_next)

    for h in range(2):
        x_high, x_low = split(xs[:, h * half : (h + 1) * half])
        t_all = mm(rth[...], x_high) + mm(rth[...], x_low) + mm(rtl[...], x_high)
        t_all = t_all.reshape(depth, rank, half)
        tf[h] = t_all
        ts[h, pl.ds(0, depth)] = t_all.astype(bf16)

    own_u = pp_ref[me]

    def weights(low_e, high_e):
        def one(e, carry):
            spot = 0
            other = 0
            for i in range(depth):
                bit = lax.rem(e // 2**i, 2)
                spot = spot + bit * 2 ** (depth - 1 - i)
                other = other + lax.rem(bit + bits[i], 2) * 2**i
            first = first_ref[other, me]
            last = first + count_ref[other, me]
            t_col = jnp.broadcast_to(mpb[e], (128, 128)).T[:tile]
            base = pl.multiple_of(spot * tile, tile)
            for b in range(rows // leaf):
                u_row = own_u[:, b * leaf : (b + 1) * leaf]
                listed = jnp.logical_and(first <= b, b < last)
                u_row = jnp.where(listed, u_row, FAR)
                scaled = jnp.minimum(jnp.abs(t_col - u_row) * (2.0 * leaf), 1.0)
                rest = 1.0 - scaled
                square = rest * rest
                value = AMPLITUDE * (square * square * (1.0 + 4.0 * scaled))
                wts[pl.ds(base, tile), b * leaf : (b + 1) * leaf] = value.astype(bf16)
            return carry

        lax.fori_loop(low_e, high_e, one, 0)

    forwards = []
    for k in range(depth):
        m = depth - 1 - k
        span = pl.ds(t_off[k], m + 1)
        if k == 0:
            t_copies = [
                remote(ts.at[1 - par, span], tr.at[span], 0),
                remote(ts.at[par, m], cbuf.at[m, par], 0),
            ]
        else:
            t_copies = [remote(ts.at[par, span], tr.at[span], k)]
        if mp_next < depth:
            mp_copy.wait_recv()
            mp_next += 1
            if mp_next < depth:
                mp_copy = start_mp(mp_next)
        if m > 0:
            g_copy.wait_recv()
            rest = pairs[m] - m
            if rest > 0:
                total = gf[g_off[k] + m : g_off[k] + pairs[m]] + gr[
                    g_off[k] + m : g_off[k] + pairs[m]
                ].astype(f32)
                gf[g_off[k + 1] : g_off[k + 1] + rest] = total
                gs[g_off[k + 1] : g_off[k + 1] + rest] = total.astype(bf16)
                g_copy = start_g(k + 1)
        if k == depth - 2:
            while mp_next < depth:
                mp_copy.wait_recv()
                mp_next += 1
                if mp_next < depth:
                    mp_copy = start_mp(mp_next)
            weights(0, n // 2)
        if k == depth - 1:
            weights(n // 2, n)
        for copy in t_copies:
            copy.wait_recv()
        if k > 0:
            forwards.append(remote(tr.at[t_off[k] + m], cbuf.at[m, par], 0))
        if m > 0:
            mine = ts[par, t_off[k] + m]
            theirs = tr[t_off[k] + m]
            g_mine = gs[g_off[k] : g_off[k] + m].reshape(m * rank, rank)
            g_theirs = gr[g_off[k] : g_off[k] + m].reshape(m * rank, rank)
            gained = mm(g_mine, theirs) + mm(g_theirs, mine)
            total = (
                tf[par, :m]
                + tr[t_off[k] : t_off[k] + m].astype(f32)
                + gained.reshape(m, rank, half)
            )
            tf[par, pl.ds(0, m)] = total
            ts[par, pl.ds(t_off[k + 1], m)] = total.astype(bf16)

    mine_cols = pl.ds(pl.multiple_of(par * half, half), half)
    other_cols = pl.ds(pl.multiple_of((1 - par) * half, half), half)

    def finish(columns, parts):
        stacked = jnp.concatenate(parts, axis=0)
        total = xs[:, columns] + mm(lh[...], stacked) + mm(ll[...], stacked)
        out_ref[:, columns] = total
        co[:, columns] = total.astype(bf16)

    finish(mine_cols, [tr[t_off[depth - 1 - m] + m] for m in range(depth)])
    for copy in forwards:
        copy.wait_recv()
    finish(other_cols, [cbuf[m, 1 - par] for m in range(depth)])

    step_rows = min(256, n // 2 * tile)
    half_rows = n // 2 * tile

    def send_part(i, carry):
        at = pl.multiple_of(i * step_rows, step_rows)
        ms[pl.ds(at, step_rows), :] = mm(
            wts[pl.ds(half_rows + at, step_rows), :], co[...]
        ).astype(bf16)
        return carry

    def keep_part(i, carry):
        at = pl.multiple_of(i * step_rows, step_rows)
        acc[pl.ds(at, step_rows), :] = mm(wts[pl.ds(at, step_rows), :], co[...])
        return carry

    lax.fori_loop(0, half_rows // step_rows, send_part, 0)
    copy = remote(ms.at[pl.ds(0, half_rows)], mr.at[pl.ds(0, half_rows)], 0)
    lax.fori_loop(0, half_rows // step_rows, keep_part, 0)
    for k in range(1, depth):
        size = n // 2 ** (k + 1) * tile
        copy.wait_recv()
        old = m_off[k - 1]
        ms[m_off[k] : m_off[k] + size, :] = (
            acc[size : 2 * size, :] + mr[old + size : old + 2 * size, :].astype(f32)
        ).astype(bf16)
        copy = remote(ms.at[pl.ds(m_off[k], size)], mr.at[pl.ds(m_off[k], size)], k)
        acc[:size, :] += mr[old : old + size, :].astype(f32)
    partial = prior_ref[...].astype(f32) + acc[:tile, :]
    copy.wait_recv()
    old = m_off[depth - 1]
    map_ref[...] = partial + mr[old : old + tile, :].astype(f32)
    for copy in started:
        copy.wait_send()


def body(
    residual_cols,
    leaf_inverse,
    basis_left,
    basis_right,
    point_pos,
    map_pos,
    prior_map,
    block_first,
    block_count,
):
    rows, samples = residual_cols.shape
    leaf = leaf_inverse.shape[1]
    levels, _, rank = basis_left.shape
    n = lax.axis_size("pts")
    depth = n.bit_length() - 1
    tile = map_pos.shape[0]
    half = samples // 2
    pair_total = sum(m * (m + 1) // 2 for m in range(depth))
    t_total = depth * (depth + 1) // 2
    vmem = pl.BlockSpec(memory_space=pltpu.VMEM)
    smem = pl.BlockSpec(memory_space=pltpu.SMEM)
    copies = 5 * depth
    return pl.pallas_call(
        functools.partial(kernel, n, leaf),
        out_shape=(
            jax.ShapeDtypeStruct((rows, samples), f32),
            jax.ShapeDtypeStruct((tile, samples), f32),
        ),
        in_specs=[vmem] * 7 + [smem] * 2,
        out_specs=(vmem, vmem),
        scratch_shapes=[
            pltpu.VMEM((rows, samples), f32),
            pltpu.VMEM((depth * rank, rows), bf16),
            pltpu.VMEM((depth * rank, rows), bf16),
            pltpu.VMEM((rows, depth * rank), bf16),
            pltpu.VMEM((rows, depth * rank), bf16),
            pltpu.VMEM((pair_total, rank, rank), f32),
            pltpu.VMEM((pair_total, rank, rank), bf16),
            pltpu.VMEM((pair_total, rank, rank), bf16),
            pltpu.VMEM((2, depth, rank, half), f32),
            pltpu.VMEM((2, t_total, rank, half), bf16),
            pltpu.VMEM((t_total, rank, half), bf16),
            pltpu.VMEM((depth, 2, rank, half), bf16),
            pltpu.VMEM((rows, samples), bf16),
            pltpu.VMEM((n, 1, 128), f32),
            pltpu.VMEM((n * tile, rows), bf16),
            pltpu.VMEM((n // 2 * tile, samples), f32),
            pltpu.VMEM((n * tile, samples), bf16),
            pltpu.VMEM((n * tile, samples), bf16),
            pltpu.SemaphoreType.DMA((copies,)),
            pltpu.SemaphoreType.DMA((copies,)),
        ],
        compiler_params=pltpu.CompilerParams(
            collective_id=0, has_side_effects=True, vmem_limit_bytes=60 * 1024 * 1024
        ),
    )(
        residual_cols,
        leaf_inverse,
        basis_left,
        basis_right,
        point_pos.reshape(n, 1, rows),
        jnp.pad(map_pos, (0, 128 - tile)).reshape(1, 1, 128),
        prior_map,
        block_first,
        block_count,
    )


def solution(mesh):
    in_specs = (
        P(("groups", "pts"), None),
        P(("groups", "pts"), None),
        P(None, ("groups", "pts"), None),
        P(None, ("groups", "pts"), None),
        P(),
        P("pts"),
        P(("groups", "pts"), None),
        P(),
        P(),
    )
    out_specs = (P(("groups", "pts"), None), P(("groups", "pts"), None))
    return jax.shard_map(body, mesh=mesh, in_specs=in_specs, out_specs=out_specs, check_vma=False)
```

```python
import functools

import jax
import jax.numpy as jnp
from jax import lax
from jax.experimental import pallas as pl
from jax.experimental.pallas import tpu as pltpu
from jax.sharding import PartitionSpec as P

AMPLITUDE = 0.2
FAR = -1e6
PIECES = 4
f32 = jnp.float32
bf16 = jnp.bfloat16


def split(value):
    high = value.astype(bf16)
    return high, (value - high.astype(f32)).astype(bf16)


def mm(a, b):
    return jnp.dot(a, b, preferred_element_type=f32)


def mm3(a, b):
    return mm(a[0], b[0]) + mm(a[0], b[1]) + mm(a[1], b[0])


def kernel(
    n,
    leaf,
    res_ref,
    inv_ref,
    bl_hbm,
    br_hbm,
    pp_ref,
    mp_ref,
    prior_ref,
    first_ref,
    count_ref,
    out_hbm,
    map_ref,
    bl_ref,
    br_ref,
    xs,
    rth,
    rtl,
    lh,
    ll,
    gf,
    gs,
    gr,
    tf,
    ts,
    tr,
    cbuf,
    co,
    mpb,
    wts,
    acc,
    ms,
    mr,
    fs,
    fr,
    ss,
    sr,
    lt,
    lr,
    send_sem,
    recv_sem,
    load_sem,
    store_sem,
):
    rows, samples = res_ref.shape
    rank = bl_ref.shape[2]
    levels = bl_ref.shape[0]
    half = samples // 2
    depth = n.bit_length() - 1
    tile = prior_ref.shape[0]
    me = lax.axis_index("pts")
    bits = [lax.rem(me // 2**k, 2) for k in range(depth)]
    partners = [me + 2**k * (1 - 2 * bits[k]) for k in range(depth)]
    par = bits[0]
    started = []

    def remote(src, dst, k):
        index = len(started)
        copy = pltpu.make_async_remote_copy(
            src_ref=src,
            dst_ref=dst,
            send_sem=send_sem.at[index],
            recv_sem=recv_sem.at[index],
            device_id={"pts": partners[k]},
            device_id_type=pl.DeviceIdType.MESH,
        )
        copy.start()
        started.append(copy)
        return copy

    order = list(range(depth)) + list(range(levels - 1, depth - 1, -1))
    loads = {}
    for l in order:
        for side, (src, dst) in enumerate(((br_hbm, br_ref), (bl_hbm, bl_ref))):
            loads[side, l] = pltpu.make_async_copy(
                src.at[l], dst.at[l], load_sem.at[side * levels + l]
            )
            loads[side, l].start()

    barrier = pltpu.get_barrier_semaphore()
    for k in range(depth):
        pl.semaphore_signal(
            barrier, inc=1, device_id={"pts": partners[k]}, device_id_type=pl.DeviceIdType.MESH
        )

    pairs = [m * (m + 1) // 2 for m in range(depth)]
    g_off, t_off = [], []
    g_at = t_at = 0
    for k in range(depth):
        m = depth - 1 - k
        g_off.append(g_at)
        t_off.append(t_at)
        g_at += pairs[m]
        t_at += m + 1

    mpb[0] = jnp.zeros((1, 128), f32)
    mpb[0, :, :tile] = mp_ref[0]
    for l in range(depth):
        loads[0, l].wait()
        loads[1, l].wait()
        high, low = split(br_ref[l].T)
        rth[l * rank : (l + 1) * rank, :] = high
        rtl[l * rank : (l + 1) * rank, :] = low
        high, low = split(bl_ref[l])
        lh[:, l * rank : (l + 1) * rank] = high
        ll[:, l * rank : (l + 1) * rank] = low
    at = 0
    for m in range(depth - 1, 0, -1):
        product = mm(rth[: m * rank, :], lh[:, m * rank : (m + 1) * rank])
        product = product.reshape(m, rank, rank)
        gf[at : at + m] = product
        gs[at : at + m] = product.astype(bf16)
        at += m

    pl.semaphore_wait(barrier, depth)

    def start_g(k):
        size = pairs[depth - 1 - k]
        view = pl.ds(g_off[k], size)
        return remote(gs.at[view], gr.at[view], k)

    def start_mp(k):
        return remote(mpb.at[pl.ds(0, 2**k)], mpb.at[pl.ds(2**k, 2**k)], k)

    g_copy = start_g(0) if depth > 1 else None
    mp_copy = start_mp(0)

    def next_g(k):
        m = depth - 1 - k
        rest = pairs[m] - m
        if rest <= 0:
            return None
        total = gf[g_off[k] + m : g_off[k] + pairs[m]] + gr[
            g_off[k] + m : g_off[k] + pairs[m]
        ].astype(f32)
        gf[g_off[k + 1] : g_off[k + 1] + rest] = total
        gs[g_off[k + 1] : g_off[k + 1] + rest] = total.astype(bf16)
        return start_g(k + 1)

    for b in range(rows // leaf):
        part = mm(inv_ref[b * leaf : (b + 1) * leaf, :], res_ref[b * leaf : (b + 1) * leaf, :])
        xs[b * leaf : (b + 1) * leaf, :] = part
    total_rows = rows * n
    for level in range(levels - 1, depth - 1, -1):
        loads[0, level].wait()
        loads[1, level].wait()
    for level in range(levels - 1, depth - 1, -1):
        size = total_rows // 2 ** (level + 1)
        count = rows // size
        projected = []
        for a in range(count):
            view = slice(a * size, (a + 1) * size)
            projected.append(split(mm3(split(br_ref[level, view, :].T), split(xs[view, :]))))
        for a in range(count):
            view = slice(a * size, (a + 1) * size)
            xs[view, :] += mm3(split(bl_ref[level, view, :]), projected[a ^ 1])

    if depth > 1:
        g_copy.wait_recv()
        g_copy = next_g(0)
    mp_copy.wait_recv()
    mp_next = 1
    if mp_next < depth:
        mp_copy = start_mp(mp_next)

    x_high, x_low = split(xs[...])
    t_all = mm(rth[...], x_high) + mm(rth[...], x_low) + mm(rtl[...], x_high)
    for h in range(2):
        t_half = t_all[:, h * half : (h + 1) * half].reshape(depth, rank, half)
        tf[h] = t_half
        ts[h, pl.ds(0, depth)] = t_half.astype(bf16)

    own_u = pp_ref[me]

    def weights(low_e, high_e):
        def one(e, carry):
            spot = 0
            other = 0
            for i in range(depth):
                bit = lax.rem(e // 2**i, 2)
                spot = spot + bit * 2 ** (depth - 1 - i)
                other = other + lax.rem(bit + bits[i], 2) * 2**i
            first = first_ref[other, me]
            last = first + count_ref[other, me]
            t_col = jnp.broadcast_to(mpb[e], (128, 128)).T[:tile]
            base = pl.multiple_of(spot * tile, tile)
            for b in range(rows // leaf):
                u_row = own_u[:, b * leaf : (b + 1) * leaf]
                listed = jnp.logical_and(first <= b, b < last)
                u_row = jnp.where(listed, u_row, FAR)
                scaled = jnp.minimum(jnp.abs(t_col - u_row) * (2.0 * leaf), 1.0)
                rest = 1.0 - scaled
                square = rest * rest
                value = AMPLITUDE * (square * square * (1.0 + 4.0 * scaled))
                wts[pl.ds(base, tile), b * leaf : (b + 1) * leaf] = value.astype(bf16)
            return carry

        lax.fori_loop(low_e, high_e, one, 0)

    forwards = []
    for k in range(depth):
        m = depth - 1 - k
        span = pl.ds(t_off[k], m + 1)
        if k == 0:
            t_copies = [
                remote(ts.at[1 - par, span], tr.at[span], 0),
                remote(ts.at[par, m], cbuf.at[m, par], 0),
            ]
        else:
            t_copies = [remote(ts.at[par, span], tr.at[span], k)]
        if mp_next < depth:
            mp_copy.wait_recv()
            mp_next += 1
            if mp_next < depth:
                mp_copy = start_mp(mp_next)
        if k > 0 and m > 0:
            g_copy.wait_recv()
            g_copy = next_g(k)
        if k == depth - 2:
            while mp_next < depth:
                mp_copy.wait_recv()
                mp_next += 1
                if mp_next < depth:
                    mp_copy = start_mp(mp_next)
            weights(0, n // 2)
        if k == depth - 1:
            weights(n // 2, n)
        for copy in t_copies:
            copy.wait_recv()
        if k > 0:
            forwards.append(remote(tr.at[t_off[k] + m], cbuf.at[m, par], 0))
        if m > 0:
            mine = ts[par, t_off[k] + m]
            theirs = tr[t_off[k] + m]
            g_mine = gs[g_off[k] : g_off[k] + m].reshape(m * rank, rank)
            g_theirs = gr[g_off[k] : g_off[k] + m].reshape(m * rank, rank)
            gained = mm(g_mine, theirs) + mm(g_theirs, mine)
            total = (
                tf[par, :m]
                + tr[t_off[k] : t_off[k] + m].astype(f32)
                + gained.reshape(m, rank, half)
            )
            tf[par, pl.ds(0, m)] = total
            ts[par, pl.ds(t_off[k + 1], m)] = total.astype(bf16)

    mine_cols = pl.ds(pl.multiple_of(par * half, half), half)
    other_cols = pl.ds(pl.multiple_of((1 - par) * half, half), half)

    def finish(columns, parts):
        stacked = jnp.concatenate(parts, axis=0)
        total = xs[:, columns] + mm(lh[...], stacked) + mm(ll[...], stacked)
        xs[:, columns] = total
        co[:, columns] = total.astype(bf16)

    finish(mine_cols, [tr[t_off[depth - 1 - m] + m] for m in range(depth)])
    for copy in forwards:
        copy.wait_recv()
    finish(other_cols, [cbuf[m, 1 - par] for m in range(depth)])

    store = pltpu.make_async_copy(xs, out_hbm, store_sem.at[0])
    store.start()

    quarter = n // 8 * tile
    half_rows = 4 * quarter
    first_copies = {}
    for j in (3, 2, 1, 0):
        low = half_rows + j * quarter
        ms[j] = mm(wts[low : low + quarter, :], co[...]).astype(bf16)
        first_copies[j] = remote(ms.at[j], mr.at[j], 0)

    def keep(j):
        part = mm(wts[j * quarter : (j + 1) * quarter, :], co[...])
        for c in range(2):
            acc[c, j] = part[:, c * half : (c + 1) * half]

    def summed(c, j):
        return acc[c, j] + mr[j, :, c * half : (c + 1) * half].astype(f32)

    keep(3)
    keep(2)
    first_copies[3].wait_recv()
    first_copies[2].wait_recv()
    fs[0, 0] = summed(0, 2).astype(bf16)
    fs[0, 1] = summed(0, 3).astype(bf16)
    copy_a = remote(fs.at[0], fr.at[0], 1)
    keep(1)
    first_copies[1].wait_recv()
    fs[1, 0] = summed(1, 1).astype(bf16)
    fs[1, 1] = summed(1, 3).astype(bf16)
    copy_b = remote(fs.at[1], fr.at[1], 2)
    keep(0)
    first_copies[0].wait_recv()
    acc[0, 1] = summed(0, 1)
    acc[1, 2] = summed(1, 2)
    acc[0, 0] = summed(0, 0)
    acc[1, 0] = summed(1, 0)
    copy_a.wait_recv()
    ss[0] = (acc[0, 1] + fr[0, 1].astype(f32)).astype(bf16)
    copy_a = remote(ss.at[0], sr.at[0], 2)
    copy_b.wait_recv()
    ss[1] = (acc[1, 2] + fr[1, 1].astype(f32)).astype(bf16)
    copy_b = remote(ss.at[1], sr.at[1], 1)
    sums = [acc[c, 0] + fr[c, 0].astype(f32) for c in range(2)]
    copy_a.wait_recv()
    copy_b.wait_recv()
    size = quarter
    for c in range(2):
        acc[c, 0] = sums[c] + sr[c].astype(f32)
    base = 0
    for k in range(3, depth):
        size = size // 2
        for c in range(2):
            lt[c, base : base + size, :] = acc[c, 0, size : 2 * size, :].astype(bf16)
        copy = remote(
            lt.at[:, pl.ds(base, size)], lr.at[:, pl.ds(base, size)], k
        )
        copy.wait_recv()
        for c in range(2):
            acc[c, 0, :size, :] += lr[c, base : base + size, :].astype(f32)
        base += size
    for c in range(2):
        cols = slice(c * half, (c + 1) * half)
        map_ref[:, cols] = prior_ref[:, cols].astype(f32) + acc[c, 0, :tile, :]
    store.wait()
    for copy in started:
        copy.wait_send()


def deliver(solved_ref, mapped_ref, out_ref, map_ref, held, spots, in_sem, out_sem):
    piece = held.shape[0] // PIECES
    moves = [(mapped_ref, spots, map_ref)]
    for i in range(PIECES):
        view = pl.ds(i * piece, piece)
        moves.append((solved_ref.at[view], held.at[view], out_ref.at[view]))
    reads = [pltpu.make_async_copy(a, b, in_sem.at[i]) for i, (a, b, _) in enumerate(moves)]
    writes = [pltpu.make_async_copy(b, c, out_sem.at[i]) for i, (_, b, c) in enumerate(moves)]
    for read in reads:
        read.start()
    for read, write in zip(reads, writes):
        read.wait()
        write.start()
    for write in writes:
        write.wait()


def body(
    residual_cols,
    leaf_inverse,
    basis_left,
    basis_right,
    point_pos,
    map_pos,
    prior_map,
    block_first,
    block_count,
):
    rows, samples = residual_cols.shape
    leaf = leaf_inverse.shape[1]
    levels, _, rank = basis_left.shape
    n = lax.axis_size("pts")
    depth = n.bit_length() - 1
    tile = map_pos.shape[0]
    half = samples // 2
    pair_total = sum(m * (m + 1) // 2 for m in range(depth))
    t_total = depth * (depth + 1) // 2
    vmem = pl.BlockSpec(memory_space=pltpu.VMEM)
    smem = pl.BlockSpec(memory_space=pltpu.SMEM)
    anywhere = pl.BlockSpec(memory_space=pl.ANY)
    copies = 5 * depth + 8
    quarter = n // 8 * tile
    solved, mapped = pl.pallas_call(
        functools.partial(kernel, n, leaf),
        out_shape=(
            jax.ShapeDtypeStruct((rows, samples), f32),
            jax.ShapeDtypeStruct((tile, samples), f32),
        ),
        in_specs=[vmem] * 2 + [anywhere] * 2 + [vmem] * 3 + [smem] * 2,
        out_specs=(anywhere, vmem),
        scratch_shapes=[
            pltpu.VMEM((levels, rows, rank), f32),
            pltpu.VMEM((levels, rows, rank), f32),
            pltpu.VMEM((rows, samples), f32),
            pltpu.VMEM((depth * rank, rows), bf16),
            pltpu.VMEM((depth * rank, rows), bf16),
            pltpu.VMEM((rows, depth * rank), bf16),
            pltpu.VMEM((rows, depth * rank), bf16),
            pltpu.VMEM((pair_total, rank, rank), f32),
            pltpu.VMEM((pair_total, rank, rank), bf16),
            pltpu.VMEM((pair_total, rank, rank), bf16),
            pltpu.VMEM((2, depth, rank, half), f32),
            pltpu.VMEM((2, t_total, rank, half), bf16),
            pltpu.VMEM((t_total, rank, half), bf16),
            pltpu.VMEM((depth, 2, rank, half), bf16),
            pltpu.VMEM((rows, samples), bf16),
            pltpu.VMEM((n, 1, 128), f32),
            pltpu.VMEM((n * tile, rows), bf16),
            pltpu.VMEM((2, 4, quarter, half), f32),
            pltpu.VMEM((4, quarter, samples), bf16),
            pltpu.VMEM((4, quarter, samples), bf16),
            pltpu.VMEM((2, 2, quarter, half), bf16),
            pltpu.VMEM((2, 2, quarter, half), bf16),
            pltpu.VMEM((2, quarter, half), bf16),
            pltpu.VMEM((2, quarter, half), bf16),
            pltpu.VMEM((2, quarter, half), bf16),
            pltpu.VMEM((2, quarter, half), bf16),
            pltpu.SemaphoreType.DMA((copies,)),
            pltpu.SemaphoreType.DMA((copies,)),
            pltpu.SemaphoreType.DMA((2 * levels,)),
            pltpu.SemaphoreType.DMA((1,)),
        ],
        compiler_params=pltpu.CompilerParams(
            collective_id=0, has_side_effects=True, vmem_limit_bytes=60 * 1024 * 1024
        ),
    )(
        residual_cols,
        leaf_inverse,
        basis_left,
        basis_right,
        point_pos.reshape(n, 1, rows),
        map_pos.reshape(1, 1, tile),
        prior_map,
        block_first,
        block_count,
    )
    return pl.pallas_call(
        deliver,
        out_shape=(
            jax.ShapeDtypeStruct((rows, samples), f32),
            jax.ShapeDtypeStruct((tile, samples), f32),
        ),
        in_specs=[anywhere] * 2,
        out_specs=(anywhere, anywhere),
        scratch_shapes=[
            pltpu.VMEM((rows, samples), f32),
            pltpu.VMEM((tile, samples), f32),
            pltpu.SemaphoreType.DMA((PIECES + 1,)),
            pltpu.SemaphoreType.DMA((PIECES + 1,)),
        ],
    )(solved, mapped)


def solution(mesh):
    in_specs = (
        P(("groups", "pts"), None),
        P(("groups", "pts"), None),
        P(None, ("groups", "pts"), None),
        P(None, ("groups", "pts"), None),
        P(),
        P("pts"),
        P(("groups", "pts"), None),
        P(),
        P(),
    )
    out_specs = (P(("groups", "pts"), None), P(("groups", "pts"), None))
    return jax.shard_map(body, mesh=mesh, in_specs=in_specs, out_specs=out_specs, check_vma=False)
```

```python
import functools

import jax
import jax.numpy as jnp
from jax import lax
from jax.experimental import pallas as pl
from jax.experimental.pallas import tpu as pltpu
from jax.sharding import PartitionSpec as P

AMPLITUDE = 0.2
FAR = -1e6
PIECES = 4
TOGETHER = 4
f32 = jnp.float32
bf16 = jnp.bfloat16


def split(value):
    high = value.astype(bf16)
    return high, (value - high.astype(f32)).astype(bf16)


def mm(a, b):
    return jnp.dot(a, b, preferred_element_type=f32)


def mm3(a, b):
    return mm(a[0], b[0]) + mm(a[0], b[1]) + mm(a[1], b[0])


def kernel(
    n,
    leaf,
    res_ref,
    inv_ref,
    bl_hbm,
    br_hbm,
    pp_ref,
    mp_ref,
    prior_ref,
    first_ref,
    count_ref,
    out_hbm,
    map_ref,
    bl_ref,
    br_ref,
    xs,
    rth,
    rtl,
    lh,
    ll,
    gf,
    gs,
    gr,
    tf,
    ts,
    tr,
    cbuf,
    co,
    mpb,
    wts,
    acc,
    ms,
    mr,
    fs,
    fr,
    ss,
    sr,
    lt,
    lr,
    send_sem,
    recv_sem,
    load_sem,
    store_sem,
):
    rows, samples = res_ref.shape
    rank = bl_ref.shape[2]
    levels = bl_ref.shape[0]
    half = samples // 2
    depth = n.bit_length() - 1
    tile = prior_ref.shape[0]
    me = lax.axis_index("pts")
    bits = [lax.rem(me // 2**k, 2) for k in range(depth)]
    partners = [me + 2**k * (1 - 2 * bits[k]) for k in range(depth)]
    par = bits[0]
    started = []

    def remote(src, dst, k):
        index = len(started)
        copy = pltpu.make_async_remote_copy(
            src_ref=src,
            dst_ref=dst,
            send_sem=send_sem.at[index],
            recv_sem=recv_sem.at[index],
            device_id={"pts": partners[k]},
            device_id_type=pl.DeviceIdType.MESH,
        )
        copy.start()
        started.append(copy)
        return copy

    order = list(range(depth)) + list(range(levels - 1, depth - 1, -1))
    loads = {}
    for l in order:
        for side, (src, dst) in enumerate(((br_hbm, br_ref), (bl_hbm, bl_ref))):
            loads[side, l] = pltpu.make_async_copy(
                src.at[l], dst.at[l], load_sem.at[side * levels + l]
            )
            loads[side, l].start()

    barrier = pltpu.get_barrier_semaphore()
    for k in range(depth):
        pl.semaphore_signal(
            barrier, inc=1, device_id={"pts": partners[k]}, device_id_type=pl.DeviceIdType.MESH
        )

    pairs = [m * (m + 1) // 2 for m in range(depth)]
    g_off, t_off = [], []
    g_at = t_at = 0
    for k in range(depth):
        m = depth - 1 - k
        g_off.append(g_at)
        t_off.append(t_at)
        g_at += pairs[m]
        t_at += m + 1

    mpb[0] = jnp.zeros((1, 128), f32)
    mpb[0, :, :tile] = mp_ref[0]
    for l in range(depth):
        loads[0, l].wait()
        loads[1, l].wait()
        high, low = split(br_ref[l].T)
        rth[l * rank : (l + 1) * rank, :] = high
        rtl[l * rank : (l + 1) * rank, :] = low
        high, low = split(bl_ref[l])
        lh[:, l * rank : (l + 1) * rank] = high
        ll[:, l * rank : (l + 1) * rank] = low
    at = 0
    for m in range(depth - 1, 0, -1):
        product = mm(rth[: m * rank, :], lh[:, m * rank : (m + 1) * rank])
        product = product.reshape(m, rank, rank)
        gf[at : at + m] = product
        gs[at : at + m] = product.astype(bf16)
        at += m

    pl.semaphore_wait(barrier, depth)

    def start_g(k):
        size = pairs[depth - 1 - k]
        view = pl.ds(g_off[k], size)
        return remote(gs.at[view], gr.at[view], k)

    def start_mp(k):
        return remote(mpb.at[pl.ds(0, 2**k)], mpb.at[pl.ds(2**k, 2**k)], k)

    g_copy = start_g(0) if depth > 1 else None
    mp_copy = start_mp(0)

    def next_g(k):
        m = depth - 1 - k
        rest = pairs[m] - m
        if rest <= 0:
            return None
        total = gf[g_off[k] + m : g_off[k] + pairs[m]] + gr[
            g_off[k] + m : g_off[k] + pairs[m]
        ].astype(f32)
        gf[g_off[k + 1] : g_off[k + 1] + rest] = total
        gs[g_off[k + 1] : g_off[k + 1] + rest] = total.astype(bf16)
        return start_g(k + 1)

    for b in range(rows // leaf):
        part = mm(inv_ref[b * leaf : (b + 1) * leaf, :], res_ref[b * leaf : (b + 1) * leaf, :])
        xs[b * leaf : (b + 1) * leaf, :] = part
    total_rows = rows * n
    for level in range(levels - 1, depth - 1, -1):
        loads[0, level].wait()
        loads[1, level].wait()
    for level in range(levels - 1, depth - 1, -1):
        size = total_rows // 2 ** (level + 1)
        count = rows // size
        projected = []
        for a in range(count):
            view = slice(a * size, (a + 1) * size)
            projected.append(split(mm3(split(br_ref[level, view, :].T), split(xs[view, :]))))
        for a in range(count):
            view = slice(a * size, (a + 1) * size)
            xs[view, :] += mm3(split(bl_ref[level, view, :]), projected[a ^ 1])

    if depth > 1:
        g_copy.wait_recv()
        g_copy = next_g(0)
    mp_copy.wait_recv()
    mp_next = 1
    if mp_next < depth:
        mp_copy = start_mp(mp_next)

    x_high, x_low = split(xs[...])
    t_all = mm(rth[...], x_high) + mm(rth[...], x_low) + mm(rtl[...], x_high)
    for h in range(2):
        t_half = t_all[:, h * half : (h + 1) * half].reshape(depth, rank, half)
        tf[h] = t_half
        ts[h, pl.ds(0, depth)] = t_half.astype(bf16)

    own_u = pp_ref[me]

    def weights(low_e, high_e):
        def one(e):
            spot = 0
            other = 0
            for i in range(depth):
                bit = lax.rem(e // 2**i, 2)
                spot = spot + bit * 2 ** (depth - 1 - i)
                other = other + lax.rem(bit + bits[i], 2) * 2**i
            first = first_ref[other, me]
            last = first + count_ref[other, me]
            t_col = jnp.broadcast_to(mpb[e], (128, 128)).T[:tile]
            base = pl.multiple_of(spot * tile, tile)
            for b in range(rows // leaf):
                u_row = own_u[:, b * leaf : (b + 1) * leaf]
                listed = jnp.logical_and(first <= b, b < last)
                u_row = jnp.where(listed, u_row, FAR)
                scaled = jnp.minimum(jnp.abs(t_col - u_row) * (2.0 * leaf), 1.0)
                rest = 1.0 - scaled
                square = rest * rest
                value = AMPLITUDE * (square * square * (1.0 + 4.0 * scaled))
                wts[pl.ds(base, tile), b * leaf : (b + 1) * leaf] = value.astype(bf16)

        def several(i, carry):
            for j in range(TOGETHER):
                one(low_e + i * TOGETHER + j)
            return carry

        lax.fori_loop(0, (high_e - low_e) // TOGETHER, several, 0)

    forwards = []
    for k in range(depth):
        m = depth - 1 - k
        span = pl.ds(t_off[k], m + 1)
        if k == 0:
            t_copies = [
                remote(ts.at[1 - par, span], tr.at[span], 0),
                remote(ts.at[par, m], cbuf.at[m, par], 0),
            ]
        else:
            t_copies = [remote(ts.at[par, span], tr.at[span], k)]
        if mp_next < depth:
            mp_copy.wait_recv()
            mp_next += 1
            if mp_next < depth:
                mp_copy = start_mp(mp_next)
        if k > 0 and m > 0:
            g_copy.wait_recv()
            g_copy = next_g(k)
        if k == depth - 2:
            while mp_next < depth:
                mp_copy.wait_recv()
                mp_next += 1
                if mp_next < depth:
                    mp_copy = start_mp(mp_next)
        late = k - (depth - 4)
        if late >= 0:
            weights(late * (n // 4), (late + 1) * (n // 4))
        for copy in t_copies:
            copy.wait_recv()
        if k > 0:
            forwards.append(remote(tr.at[t_off[k] + m], cbuf.at[m, par], 0))
        if m > 0:
            mine = ts[par, t_off[k] + m]
            theirs = tr[t_off[k] + m]
            g_mine = gs[g_off[k] : g_off[k] + m].reshape(m * rank, rank)
            g_theirs = gr[g_off[k] : g_off[k] + m].reshape(m * rank, rank)
            gained = mm(g_mine, theirs) + mm(g_theirs, mine)
            total = (
                tf[par, :m]
                + tr[t_off[k] : t_off[k] + m].astype(f32)
                + gained.reshape(m, rank, half)
            )
            tf[par, pl.ds(0, m)] = total
            ts[par, pl.ds(t_off[k + 1], m)] = total.astype(bf16)

    mine_cols = pl.ds(pl.multiple_of(par * half, half), half)
    other_cols = pl.ds(pl.multiple_of((1 - par) * half, half), half)

    def finish(columns, parts):
        stacked = jnp.concatenate(parts, axis=0)
        total = xs[:, columns] + mm(lh[...], stacked) + mm(ll[...], stacked)
        xs[:, columns] = total
        co[:, columns] = total.astype(bf16)

    finish(mine_cols, [tr[t_off[depth - 1 - m] + m] for m in range(depth)])
    for copy in forwards:
        copy.wait_recv()
    finish(other_cols, [cbuf[m, 1 - par] for m in range(depth)])

    store = pltpu.make_async_copy(xs, out_hbm, store_sem.at[0])
    store.start()

    quarter = n // 8 * tile
    half_rows = 4 * quarter
    first_copies = {}
    for j in (3, 2, 1, 0):
        low = half_rows + j * quarter
        ms[j] = mm(wts[low : low + quarter, :], co[...]).astype(bf16)
        first_copies[j] = remote(ms.at[j], mr.at[j], 0)

    def keep(j):
        part = mm(wts[j * quarter : (j + 1) * quarter, :], co[...])
        for c in range(2):
            acc[c, j] = part[:, c * half : (c + 1) * half]

    def summed(c, j):
        return acc[c, j] + mr[j, :, c * half : (c + 1) * half].astype(f32)

    keep(3)
    keep(2)
    first_copies[3].wait_recv()
    first_copies[2].wait_recv()
    fs[0, 0] = summed(0, 2).astype(bf16)
    fs[0, 1] = summed(0, 3).astype(bf16)
    copy_a = remote(fs.at[0], fr.at[0], 1)
    keep(1)
    first_copies[1].wait_recv()
    fs[1, 0] = summed(1, 1).astype(bf16)
    fs[1, 1] = summed(1, 3).astype(bf16)
    copy_b = remote(fs.at[1], fr.at[1], 2)
    keep(0)
    first_copies[0].wait_recv()
    acc[0, 1] = summed(0, 1)
    acc[1, 2] = summed(1, 2)
    acc[0, 0] = summed(0, 0)
    acc[1, 0] = summed(1, 0)
    copy_a.wait_recv()
    ss[0] = (acc[0, 1] + fr[0, 1].astype(f32)).astype(bf16)
    copy_a = remote(ss.at[0], sr.at[0], 2)
    copy_b.wait_recv()
    ss[1] = (acc[1, 2] + fr[1, 1].astype(f32)).astype(bf16)
    copy_b = remote(ss.at[1], sr.at[1], 1)
    sums = [acc[c, 0] + fr[c, 0].astype(f32) for c in range(2)]
    copy_a.wait_recv()
    copy_b.wait_recv()
    size = quarter
    for c in range(2):
        acc[c, 0] = sums[c] + sr[c].astype(f32)
    base = 0
    for k in range(3, depth):
        size = size // 2
        for c in range(2):
            lt[c, base : base + size, :] = acc[c, 0, size : 2 * size, :].astype(bf16)
        copy = remote(
            lt.at[:, pl.ds(base, size)], lr.at[:, pl.ds(base, size)], k
        )
        copy.wait_recv()
        for c in range(2):
            acc[c, 0, :size, :] += lr[c, base : base + size, :].astype(f32)
        base += size
    for c in range(2):
        cols = slice(c * half, (c + 1) * half)
        map_ref[:, cols] = prior_ref[:, cols].astype(f32) + acc[c, 0, :tile, :]
    store.wait()
    for copy in started:
        copy.wait_send()


def deliver(solved_ref, mapped_ref, out_ref, map_ref, held, spots, in_sem, out_sem):
    piece = held.shape[0] // PIECES
    moves = [(mapped_ref, spots, map_ref)]
    for i in range(PIECES):
        view = pl.ds(i * piece, piece)
        moves.append((solved_ref.at[view], held.at[view], out_ref.at[view]))
    reads = [pltpu.make_async_copy(a, b, in_sem.at[i]) for i, (a, b, _) in enumerate(moves)]
    writes = [pltpu.make_async_copy(b, c, out_sem.at[i]) for i, (_, b, c) in enumerate(moves)]
    for read in reads:
        read.start()
    for read, write in zip(reads, writes):
        read.wait()
        write.start()
    for write in writes:
        write.wait()


def body(
    residual_cols,
    leaf_inverse,
    basis_left,
    basis_right,
    point_pos,
    map_pos,
    prior_map,
    block_first,
    block_count,
):
    rows, samples = residual_cols.shape
    leaf = leaf_inverse.shape[1]
    levels, _, rank = basis_left.shape
    n = lax.axis_size("pts")
    depth = n.bit_length() - 1
    tile = map_pos.shape[0]
    half = samples // 2
    pair_total = sum(m * (m + 1) // 2 for m in range(depth))
    t_total = depth * (depth + 1) // 2
    vmem = pl.BlockSpec(memory_space=pltpu.VMEM)
    smem = pl.BlockSpec(memory_space=pltpu.SMEM)
    anywhere = pl.BlockSpec(memory_space=pl.ANY)
    copies = 5 * depth + 8
    quarter = n // 8 * tile
    solved, mapped = pl.pallas_call(
        functools.partial(kernel, n, leaf),
        out_shape=(
            jax.ShapeDtypeStruct((rows, samples), f32),
            jax.ShapeDtypeStruct((tile, samples), f32),
        ),
        in_specs=[vmem] * 2 + [anywhere] * 2 + [vmem] * 3 + [smem] * 2,
        out_specs=(anywhere, vmem),
        scratch_shapes=[
            pltpu.VMEM((levels, rows, rank), f32),
            pltpu.VMEM((levels, rows, rank), f32),
            pltpu.VMEM((rows, samples), f32),
            pltpu.VMEM((depth * rank, rows), bf16),
            pltpu.VMEM((depth * rank, rows), bf16),
            pltpu.VMEM((rows, depth * rank), bf16),
            pltpu.VMEM((rows, depth * rank), bf16),
            pltpu.VMEM((pair_total, rank, rank), f32),
            pltpu.VMEM((pair_total, rank, rank), bf16),
            pltpu.VMEM((pair_total, rank, rank), bf16),
            pltpu.VMEM((2, depth, rank, half), f32),
            pltpu.VMEM((2, t_total, rank, half), bf16),
            pltpu.VMEM((t_total, rank, half), bf16),
            pltpu.VMEM((depth, 2, rank, half), bf16),
            pltpu.VMEM((rows, samples), bf16),
            pltpu.VMEM((n, 1, 128), f32),
            pltpu.VMEM((n * tile, rows), bf16),
            pltpu.VMEM((2, 4, quarter, half), f32),
            pltpu.VMEM((4, quarter, samples), bf16),
            pltpu.VMEM((4, quarter, samples), bf16),
            pltpu.VMEM((2, 2, quarter, half), bf16),
            pltpu.VMEM((2, 2, quarter, half), bf16),
            pltpu.VMEM((2, quarter, half), bf16),
            pltpu.VMEM((2, quarter, half), bf16),
            pltpu.VMEM((2, quarter, half), bf16),
            pltpu.VMEM((2, quarter, half), bf16),
            pltpu.SemaphoreType.DMA((copies,)),
            pltpu.SemaphoreType.DMA((copies,)),
            pltpu.SemaphoreType.DMA((2 * levels,)),
            pltpu.SemaphoreType.DMA((1,)),
        ],
        compiler_params=pltpu.CompilerParams(
            collective_id=0, has_side_effects=True, vmem_limit_bytes=60 * 1024 * 1024
        ),
    )(
        residual_cols,
        leaf_inverse,
        basis_left,
        basis_right,
        point_pos.reshape(n, 1, rows),
        map_pos.reshape(1, 1, tile),
        prior_map,
        block_first,
        block_count,
    )
    return pl.pallas_call(
        deliver,
        out_shape=(
            jax.ShapeDtypeStruct((rows, samples), f32),
            jax.ShapeDtypeStruct((tile, samples), f32),
        ),
        in_specs=[anywhere] * 2,
        out_specs=(anywhere, anywhere),
        scratch_shapes=[
            pltpu.VMEM((rows, samples), f32),
            pltpu.VMEM((tile, samples), f32),
            pltpu.SemaphoreType.DMA((PIECES + 1,)),
            pltpu.SemaphoreType.DMA((PIECES + 1,)),
        ],
    )(solved, mapped)


def solution(mesh):
    in_specs = (
        P(("groups", "pts"), None),
        P(("groups", "pts"), None),
        P(None, ("groups", "pts"), None),
        P(None, ("groups", "pts"), None),
        P(),
        P("pts"),
        P(("groups", "pts"), None),
        P(),
        P(),
    )
    out_specs = (P(("groups", "pts"), None), P(("groups", "pts"), None))
    return jax.shard_map(body, mesh=mesh, in_specs=in_specs, out_specs=out_specs, check_vma=False)
```

```python
import functools

import jax
import jax.numpy as jnp
from jax import lax
from jax.experimental import pallas as pl
from jax.experimental.pallas import tpu as pltpu
from jax.sharding import PartitionSpec as P

AMPLITUDE = 0.2
FAR = -1e6
PIECES = 4
TOGETHER = 4
f32 = jnp.float32
bf16 = jnp.bfloat16


def split(value):
    high = value.astype(bf16)
    return high, (value - high.astype(f32)).astype(bf16)


def mm(a, b):
    return jnp.dot(a, b, preferred_element_type=f32)


def mm3(a, b):
    return mm(a[0], b[0]) + mm(a[0], b[1]) + mm(a[1], b[0])


def kernel(
    n,
    leaf,
    res_ref,
    inv_ref,
    bl_hbm,
    br_hbm,
    pp_ref,
    mp_ref,
    prior_ref,
    first_ref,
    count_ref,
    out_hbm,
    map_ref,
    bl_ref,
    br_ref,
    xs,
    rth,
    rtl,
    lh,
    ll,
    gf,
    gs,
    gr,
    tf,
    ts,
    tr,
    cbuf,
    co,
    mpb,
    wts,
    acc,
    ms,
    mr,
    fs,
    fr,
    ss,
    sr,
    lt,
    lr,
    send_sem,
    recv_sem,
    load_sem,
    store_sem,
):
    rows, samples = res_ref.shape
    rank = bl_ref.shape[2]
    levels = bl_ref.shape[0]
    half = samples // 2
    depth = n.bit_length() - 1
    tile = prior_ref.shape[0]
    me = lax.axis_index("pts")
    bits = [lax.rem(me // 2**k, 2) for k in range(depth)]
    partners = [me + 2**k * (1 - 2 * bits[k]) for k in range(depth)]
    par = bits[0]
    started = []

    def remote(src, dst, k):
        index = len(started)
        copy = pltpu.make_async_remote_copy(
            src_ref=src,
            dst_ref=dst,
            send_sem=send_sem.at[index],
            recv_sem=recv_sem.at[index],
            device_id={"pts": partners[k]},
            device_id_type=pl.DeviceIdType.MESH,
        )
        copy.start()
        started.append(copy)
        return copy

    order = list(range(depth)) + list(range(levels - 1, depth - 1, -1))
    loads = {}
    for l in order:
        for side, (src, dst) in enumerate(((br_hbm, br_ref), (bl_hbm, bl_ref))):
            loads[side, l] = pltpu.make_async_copy(
                src.at[l], dst.at[l], load_sem.at[side * levels + l]
            )
            loads[side, l].start()

    barrier = pltpu.get_barrier_semaphore()
    for k in range(depth):
        pl.semaphore_signal(
            barrier, inc=1, device_id={"pts": partners[k]}, device_id_type=pl.DeviceIdType.MESH
        )

    pairs = [m * (m + 1) // 2 for m in range(depth)]
    g_off, t_off = [], []
    g_at = t_at = 0
    for k in range(depth):
        m = depth - 1 - k
        g_off.append(g_at)
        t_off.append(t_at)
        g_at += pairs[m]
        t_at += m + 1

    mpb[0] = jnp.zeros((1, 128), f32)
    mpb[0, :, :tile] = mp_ref[0]
    for l in range(depth):
        loads[0, l].wait()
        loads[1, l].wait()
        high, low = split(br_ref[l].T)
        rth[l * rank : (l + 1) * rank, :] = high
        rtl[l * rank : (l + 1) * rank, :] = low
        high, low = split(bl_ref[l])
        lh[:, l * rank : (l + 1) * rank] = high
        ll[:, l * rank : (l + 1) * rank] = low
    at = 0
    for m in range(depth - 1, 0, -1):
        product = mm(rth[: m * rank, :], lh[:, m * rank : (m + 1) * rank])
        product = product.reshape(m, rank, rank)
        gf[at : at + m] = product
        gs[at : at + m] = product.astype(bf16)
        at += m

    pl.semaphore_wait(barrier, depth)

    def start_g(k):
        m = depth - 1 - k
        rest = pairs[m] - m
        copies = []
        if rest > 0:
            view = pl.ds(g_off[k] + m, rest)
            copies.append(remote(gs.at[view], gr.at[view], k))
        view = pl.ds(g_off[k], m)
        copies.append(remote(gs.at[view], gr.at[view], k))
        return copies

    def start_mp(k):
        return remote(mpb.at[pl.ds(0, 2**k)], mpb.at[pl.ds(2**k, 2**k)], k)

    g_heads = {0: start_g(0)} if depth > 1 else {}
    mp_copy = start_mp(0)

    def next_g(k):
        m = depth - 1 - k
        rest = pairs[m] - m
        if rest <= 0:
            return None
        g_heads[k][0].wait_recv()
        total = gf[g_off[k] + m : g_off[k] + pairs[m]] + gr[
            g_off[k] + m : g_off[k] + pairs[m]
        ].astype(f32)
        gf[g_off[k + 1] : g_off[k + 1] + rest] = total
        gs[g_off[k + 1] : g_off[k + 1] + rest] = total.astype(bf16)
        g_heads[k + 1] = start_g(k + 1)
        return None

    for b in range(rows // leaf):
        part = mm(inv_ref[b * leaf : (b + 1) * leaf, :], res_ref[b * leaf : (b + 1) * leaf, :])
        xs[b * leaf : (b + 1) * leaf, :] = part
    total_rows = rows * n
    for level in range(levels - 1, depth - 1, -1):
        loads[0, level].wait()
        loads[1, level].wait()
    for level in range(levels - 1, depth - 1, -1):
        size = total_rows // 2 ** (level + 1)
        count = rows // size
        projected = []
        for a in range(count):
            view = slice(a * size, (a + 1) * size)
            projected.append(split(mm3(split(br_ref[level, view, :].T), split(xs[view, :]))))
        for a in range(count):
            view = slice(a * size, (a + 1) * size)
            xs[view, :] += mm3(split(bl_ref[level, view, :]), projected[a ^ 1])

    if depth > 1:
        next_g(0)
    mp_copy.wait_recv()
    mp_next = 1
    if mp_next < depth:
        mp_copy = start_mp(mp_next)

    x_high, x_low = split(xs[...])
    t_all = mm(rth[...], x_high) + mm(rth[...], x_low) + mm(rtl[...], x_high)
    for h in range(2):
        t_half = t_all[:, h * half : (h + 1) * half].reshape(depth, rank, half)
        tf[h] = t_half
        ts[h, pl.ds(0, depth)] = t_half.astype(bf16)

    own_u = pp_ref[me]

    def weights(low_e, high_e):
        def one(e):
            spot = 0
            other = 0
            for i in range(depth):
                bit = lax.rem(e // 2**i, 2)
                spot = spot + bit * 2 ** (depth - 1 - i)
                other = other + lax.rem(bit + bits[i], 2) * 2**i
            first = first_ref[other, me]
            last = first + count_ref[other, me]
            t_col = jnp.broadcast_to(mpb[e], (128, 128)).T[:tile]
            base = pl.multiple_of(spot * tile, tile)
            for b in range(rows // leaf):
                u_row = own_u[:, b * leaf : (b + 1) * leaf]
                listed = jnp.logical_and(first <= b, b < last)
                u_row = jnp.where(listed, u_row, FAR)
                scaled = jnp.minimum(jnp.abs(t_col - u_row) * (2.0 * leaf), 1.0)
                rest = 1.0 - scaled
                square = rest * rest
                value = AMPLITUDE * (square * square * (1.0 + 4.0 * scaled))
                wts[pl.ds(base, tile), b * leaf : (b + 1) * leaf] = value.astype(bf16)

        def several(i, carry):
            for j in range(TOGETHER):
                one(low_e + i * TOGETHER + j)
            return carry

        lax.fori_loop(0, (high_e - low_e) // TOGETHER, several, 0)

    forwards = []
    for k in range(depth):
        m = depth - 1 - k
        span = pl.ds(t_off[k], m + 1)
        if k == 0:
            t_copies = [
                remote(ts.at[1 - par, span], tr.at[span], 0),
                remote(ts.at[par, m], cbuf.at[m, par], 0),
            ]
        else:
            t_copies = [remote(ts.at[par, span], tr.at[span], k)]
        if mp_next < depth:
            mp_copy.wait_recv()
            mp_next += 1
            if mp_next < depth:
                mp_copy = start_mp(mp_next)
        if k > 0 and m > 0:
            next_g(k)
        if k == depth - 2:
            while mp_next < depth:
                mp_copy.wait_recv()
                mp_next += 1
                if mp_next < depth:
                    mp_copy = start_mp(mp_next)
        late = k - (depth - 4)
        if late >= 0:
            weights(late * (n // 4), (late + 1) * (n // 4))
        for copy in t_copies:
            copy.wait_recv()
        if k > 0:
            forwards.append(remote(tr.at[t_off[k] + m], cbuf.at[m, par], 0))
        if m > 0:
            g_heads[k][-1].wait_recv()
            mine = ts[par, t_off[k] + m]
            theirs = tr[t_off[k] + m]
            g_mine = gs[g_off[k] : g_off[k] + m].reshape(m * rank, rank)
            g_theirs = gr[g_off[k] : g_off[k] + m].reshape(m * rank, rank)
            gained = mm(g_mine, theirs) + mm(g_theirs, mine)
            total = (
                tf[par, :m]
                + tr[t_off[k] : t_off[k] + m].astype(f32)
                + gained.reshape(m, rank, half)
            )
            tf[par, pl.ds(0, m)] = total
            ts[par, pl.ds(t_off[k + 1], m)] = total.astype(bf16)

    mine_cols = pl.ds(pl.multiple_of(par * half, half), half)
    other_cols = pl.ds(pl.multiple_of((1 - par) * half, half), half)

    def finish(columns, parts):
        stacked = jnp.concatenate(parts, axis=0)
        total = xs[:, columns] + mm(lh[...], stacked) + mm(ll[...], stacked)
        xs[:, columns] = total
        co[:, columns] = total.astype(bf16)

    finish(mine_cols, [tr[t_off[depth - 1 - m] + m] for m in range(depth)])
    for copy in forwards:
        copy.wait_recv()
    finish(other_cols, [cbuf[m, 1 - par] for m in range(depth)])

    store = pltpu.make_async_copy(xs, out_hbm, store_sem.at[0])
    store.start()

    quarter = n // 8 * tile
    half_rows = 4 * quarter
    first_copies = {}
    for j in (3, 2, 1, 0):
        low = half_rows + j * quarter
        ms[j] = mm(wts[low : low + quarter, :], co[...]).astype(bf16)
        first_copies[j] = remote(ms.at[j], mr.at[j], 0)

    def keep(j):
        part = mm(wts[j * quarter : (j + 1) * quarter, :], co[...])
        for c in range(2):
            acc[c, j] = part[:, c * half : (c + 1) * half]

    def summed(c, j):
        return acc[c, j] + mr[j, :, c * half : (c + 1) * half].astype(f32)

    keep(3)
    keep(2)
    first_copies[3].wait_recv()
    first_copies[2].wait_recv()
    fs[0, 0] = summed(0, 2).astype(bf16)
    fs[0, 1] = summed(0, 3).astype(bf16)
    copy_a = remote(fs.at[0], fr.at[0], 1)
    keep(1)
    first_copies[1].wait_recv()
    fs[1, 0] = summed(1, 1).astype(bf16)
    fs[1, 1] = summed(1, 3).astype(bf16)
    copy_b = remote(fs.at[1], fr.at[1], 2)
    keep(0)
    first_copies[0].wait_recv()
    acc[0, 1] = summed(0, 1)
    acc[1, 2] = summed(1, 2)
    acc[0, 0] = summed(0, 0)
    acc[1, 0] = summed(1, 0)
    copy_a.wait_recv()
    ss[0] = (acc[0, 1] + fr[0, 1].astype(f32)).astype(bf16)
    copy_a = remote(ss.at[0], sr.at[0], 2)
    copy_b.wait_recv()
    ss[1] = (acc[1, 2] + fr[1, 1].astype(f32)).astype(bf16)
    copy_b = remote(ss.at[1], sr.at[1], 1)
    sums = [acc[c, 0] + fr[c, 0].astype(f32) for c in range(2)]
    copy_a.wait_recv()
    copy_b.wait_recv()
    size = quarter
    for c in range(2):
        acc[c, 0] = sums[c] + sr[c].astype(f32)
    base = 0
    for k in range(3, depth):
        size = size // 2
        for c in range(2):
            lt[c, base : base + size, :] = acc[c, 0, size : 2 * size, :].astype(bf16)
        copy = remote(
            lt.at[:, pl.ds(base, size)], lr.at[:, pl.ds(base, size)], k
        )
        copy.wait_recv()
        for c in range(2):
            acc[c, 0, :size, :] += lr[c, base : base + size, :].astype(f32)
        base += size
    for c in range(2):
        cols = slice(c * half, (c + 1) * half)
        map_ref[:, cols] = prior_ref[:, cols].astype(f32) + acc[c, 0, :tile, :]
    store.wait()
    for copy in started:
        copy.wait_send()


def deliver(solved_ref, mapped_ref, out_ref, map_ref, held, spots, in_sem, out_sem):
    piece = held.shape[0] // PIECES
    moves = [(mapped_ref, spots, map_ref)]
    for i in range(PIECES):
        view = pl.ds(i * piece, piece)
        moves.append((solved_ref.at[view], held.at[view], out_ref.at[view]))
    reads = [pltpu.make_async_copy(a, b, in_sem.at[i]) for i, (a, b, _) in enumerate(moves)]
    writes = [pltpu.make_async_copy(b, c, out_sem.at[i]) for i, (_, b, c) in enumerate(moves)]
    for read in reads:
        read.start()
    for read, write in zip(reads, writes):
        read.wait()
        write.start()
    for write in writes:
        write.wait()


def body(
    residual_cols,
    leaf_inverse,
    basis_left,
    basis_right,
    point_pos,
    map_pos,
    prior_map,
    block_first,
    block_count,
):
    rows, samples = residual_cols.shape
    leaf = leaf_inverse.shape[1]
    levels, _, rank = basis_left.shape
    n = lax.axis_size("pts")
    depth = n.bit_length() - 1
    tile = map_pos.shape[0]
    half = samples // 2
    pair_total = sum(m * (m + 1) // 2 for m in range(depth))
    t_total = depth * (depth + 1) // 2
    vmem = pl.BlockSpec(memory_space=pltpu.VMEM)
    smem = pl.BlockSpec(memory_space=pltpu.SMEM)
    anywhere = pl.BlockSpec(memory_space=pl.ANY)
    copies = 6 * depth + 8
    quarter = n // 8 * tile
    solved, mapped = pl.pallas_call(
        functools.partial(kernel, n, leaf),
        out_shape=(
            jax.ShapeDtypeStruct((rows, samples), f32),
            jax.ShapeDtypeStruct((tile, samples), f32),
        ),
        in_specs=[vmem] * 2 + [anywhere] * 2 + [vmem] * 3 + [smem] * 2,
        out_specs=(anywhere, vmem),
        scratch_shapes=[
            pltpu.VMEM((levels, rows, rank), f32),
            pltpu.VMEM((levels, rows, rank), f32),
            pltpu.VMEM((rows, samples), f32),
            pltpu.VMEM((depth * rank, rows), bf16),
            pltpu.VMEM((depth * rank, rows), bf16),
            pltpu.VMEM((rows, depth * rank), bf16),
            pltpu.VMEM((rows, depth * rank), bf16),
            pltpu.VMEM((pair_total, rank, rank), f32),
            pltpu.VMEM((pair_total, rank, rank), bf16),
            pltpu.VMEM((pair_total, rank, rank), bf16),
            pltpu.VMEM((2, depth, rank, half), f32),
            pltpu.VMEM((2, t_total, rank, half), bf16),
            pltpu.VMEM((t_total, rank, half), bf16),
            pltpu.VMEM((depth, 2, rank, half), bf16),
            pltpu.VMEM((rows, samples), bf16),
            pltpu.VMEM((n, 1, 128), f32),
            pltpu.VMEM((n * tile, rows), bf16),
            pltpu.VMEM((2, 4, quarter, half), f32),
            pltpu.VMEM((4, quarter, samples), bf16),
            pltpu.VMEM((4, quarter, samples), bf16),
            pltpu.VMEM((2, 2, quarter, half), bf16),
            pltpu.VMEM((2, 2, quarter, half), bf16),
            pltpu.VMEM((2, quarter, half), bf16),
            pltpu.VMEM((2, quarter, half), bf16),
            pltpu.VMEM((2, quarter, half), bf16),
            pltpu.VMEM((2, quarter, half), bf16),
            pltpu.SemaphoreType.DMA((copies,)),
            pltpu.SemaphoreType.DMA((copies,)),
            pltpu.SemaphoreType.DMA((2 * levels,)),
            pltpu.SemaphoreType.DMA((1,)),
        ],
        compiler_params=pltpu.CompilerParams(
            collective_id=0, has_side_effects=True, vmem_limit_bytes=60 * 1024 * 1024
        ),
    )(
        residual_cols,
        leaf_inverse,
        basis_left,
        basis_right,
        point_pos.reshape(n, 1, rows),
        map_pos.reshape(1, 1, tile),
        prior_map,
        block_first,
        block_count,
    )
    return pl.pallas_call(
        deliver,
        out_shape=(
            jax.ShapeDtypeStruct((rows, samples), f32),
            jax.ShapeDtypeStruct((tile, samples), f32),
        ),
        in_specs=[anywhere] * 2,
        out_specs=(anywhere, anywhere),
        scratch_shapes=[
            pltpu.VMEM((rows, samples), f32),
            pltpu.VMEM((tile, samples), f32),
            pltpu.SemaphoreType.DMA((PIECES + 1,)),
            pltpu.SemaphoreType.DMA((PIECES + 1,)),
        ],
    )(solved, mapped)


def solution(mesh):
    in_specs = (
        P(("groups", "pts"), None),
        P(("groups", "pts"), None),
        P(None, ("groups", "pts"), None),
        P(None, ("groups", "pts"), None),
        P(),
        P("pts"),
        P(("groups", "pts"), None),
        P(),
        P(),
    )
    out_specs = (P(("groups", "pts"), None), P(("groups", "pts"), None))
    return jax.shard_map(body, mesh=mesh, in_specs=in_specs, out_specs=out_specs, check_vma=False)
```
